32 devices in a mesh: rows: 4 (over y, x), cols: 8 (over z, core).
Axes of the slice: x: 2, y: 2, z: 4, core: 2. Of those that a mesh axis runs over, the one named last changes fastest.
Arguments:
- counts: bfloat16 [2048, 65536], P('rows', 'cols'), may hold values from 0 to 12, as said below
- start_a: float32 [2048, 128], P(('rows', 'cols')), may hold values from -0.4 to 0.4
- start_b: float32 [4096, 128], P(('cols', 'rows')), may hold values from -0.4 to 0.4
- start_c: float32 [16, 128], replicated, may hold values from -0.4 to 0.4
Outputs:
- factor_a: float32 [2048, 128], P(('rows', 'cols'))
- factor_b: float32 [4096, 128], P(('cols', 'rows'))
- factor_c: float32 [16, 128], replicated
The draws below stay inside these ranges and needn't reach their ends.
Inputs may be any that keep to these rules, and one draw needn't show every extreme that they name: counts holds whole numbers.
All inputs are finite; a program needn't handle non-finite values.
Results may differ from the reference program's by a relative error of at most 0.009.
Values may be sent and summed in bfloat16 or wider, within the bound.
A program may use at most 128 MiB of HBM per device.

```python
import math
import jax
import jax.numpy as jnp
from jax import lax

R = 128
K = 16
ITERS = 2
I = 2048
J = 4096


def draw_counts(key, part):
    keys = jax.random.split(key, 4)
    rate_first = jax.random.randint(keys[0], (I, 1, 1), 0, 5)
    rate_second = jax.random.randint(keys[1], (1, J, 1), 0, 5)
    rate_third = jax.random.randint(keys[2], (1, 1, K), 0, 5)
    ceiling = 1 + rate_first + rate_second + rate_third
    values = jax.random.randint(keys[3], (I, J, K), 0, ceiling)
    values = values.at[0, 0, 0].set(12)
    return values.reshape(I, J * K).astype(jnp.float32).astype(jnp.bfloat16)


def shard_levels(key, shape, shards, least, top_value):
    factor_of = 1.0
    for position, blocks in shards:
        steps = jax.random.uniform(jax.random.fold_in(jax.random.fold_in(key, 6), position), (blocks,), jnp.float32, least / len(shards), top_value / len(shards))
        factor_of = factor_of * jnp.repeat(jnp.exp(steps), shape[position] // blocks).reshape((-1,) + (1,) * (len(shape) - 1 - position))
    return factor_of


def setup_inputs(seed: int = 0) -> dict:
    seeds = jax.random.split(jax.random.key(seed), 5)
    counts = draw_counts(jax.random.fold_in(seeds[4], 71), 0)
    start_a = jnp.clip(jax.random.uniform(seeds[1], (I, R), jnp.float32, -0.4, 0.4) * shard_levels(seeds[1], (I, R), ((0, 32),), -0.4, 0.0), -0.4, 0.4)
    start_b = jnp.clip(jax.random.uniform(seeds[2], (J, R), jnp.float32, -0.4, 0.4) * shard_levels(seeds[2], (J, R), ((0, 32),), -0.4, 0.0), -0.4, 0.4)
    start_c = jnp.clip(jax.random.uniform(seeds[3], (K, R), jnp.float32, -0.4, 0.4), -0.4, 0.4)
    return {"counts": counts, "start_a": start_a, "start_b": start_b, "start_c": start_c}


def one_step(counts, whole_a, whole_b, whole_c):
    low_a = whole_a.astype(jnp.bfloat16)
    low_b = whole_b.astype(jnp.bfloat16)
    scaled = (low_b.astype(jnp.float32)[:, None, :] * whole_c[None, :, :]).astype(jnp.bfloat16)
    scaled = scaled.reshape(J * K, R)
    block_rows = math.gcd(I, 256)
    flat = counts.reshape(I // block_rows, block_rows, J * K)
    blocks_a = low_a.reshape(I // block_rows, block_rows, R)

    def visit(mixed, pair):
        values, rows_a = pair
        log_rate = lax.dot_general(rows_a, scaled, (((1,), (1,)), ((), ())), preferred_element_type=jnp.float32)
        residual = (jnp.exp(log_rate) - values.astype(jnp.float32)).astype(jnp.bfloat16)
        grad_rows = jnp.dot(residual, scaled, preferred_element_type=jnp.float32)
        mixed = mixed + lax.dot_general(residual, rows_a, (((0,), (0,)), ((), ())), preferred_element_type=jnp.float32)
        return (mixed, grad_rows)
    mixed, grad_a = lax.scan(visit, jnp.zeros((J * K, R), jnp.float32), (flat, blocks_a))
    grad_a = grad_a.reshape(I, R)
    mixed = mixed.reshape(J, K, R)
    grad_b = lax.optimization_barrier(jnp.sum(mixed * whole_c[None, :, :], axis=1))
    grad_c = lax.optimization_barrier(jnp.sum(mixed * low_b.astype(jnp.float32)[:, None, :], axis=0))
    whole_a = whole_a - 0.3 / math.sqrt(J * K) * grad_a
    whole_b = whole_b - 0.3 / math.sqrt(I * K) * grad_b
    whole_c = whole_c - 0.3 / math.sqrt(I * J) * grad_c
    return (whole_a, whole_b, whole_c)

def reference(counts, start_a, start_b, start_c):
    whole_a, whole_b, whole_c = (start_a, start_b, start_c)
    for iteration in range(ITERS):
        whole_a, whole_b, whole_c = one_step(counts, whole_a, whole_b, whole_c)
    return (whole_a, whole_b, whole_c)
```

```python
import functools
import math

import jax
import jax.numpy as jnp
from jax import lax
from jax.experimental import pallas as pl
from jax.experimental.pallas import tpu as pltpu
from jax.sharding import PartitionSpec as P

ITERS = 2
MESH = pl.DeviceIdType.MESH
F32 = jnp.float32
BF16 = jnp.bfloat16


def kernel(nr, nc, tile, rates, counts_hbm, a_hbm, b_hbm, c_hbm, a_out, b_out, c_out,
           a_in, b_in, c_in, in_sem, counts, all_a, all_b, send_a, send_b, recv_a, recv_b, part_c, sum_c,
           held_a, trans_a, acc_a, acc_c, resid, scaled, mixed_t, grad_b,
           cnt_sem, ag_send, ag_recv, bg_send, bg_recv, ar_send, ar_recv, br_send, br_recv,
           c1_send, c1_recv, c2_send, c2_recv):
    row, col = lax.axis_index("rows"), lax.axis_index("cols")
    rate_a, rate_b, rate_c = rates
    own_a, rank = a_in.shape
    own_b = b_in.shape[0]
    depth = c_in.shape[0]
    tiles = counts.shape[1]
    per = tiles // nr
    width = tile // depth

    half = nc // 2
    near, spot = lax.div(col, half), lax.rem(col, half)
    near_peers = [near * half + lax.rem(spot + off, half) for off in range(1, half)]
    far_peers = [(1 - near) * half + lax.rem(spot + off, half) for off in range(half)]
    col_peers = near_peers + far_peers
    row_peers = [lax.rem(row + off, nr) for off in range(1, nr)]
    half_rows = half * own_a

    def load(h, t):
        return pltpu.make_async_copy(
            counts_hbm.at[pl.ds(pl.multiple_of(h * half_rows, half_rows), half_rows),
                          pl.ds(pl.multiple_of(t * tile, tile), tile)],
            counts.at[h, t], cnt_sem.at[h, t])

    def chunk(side, d):
        return lax.rem(row + side + d, nr)

    barrier = pltpu.get_barrier_semaphore()
    for p in col_peers:
        pl.semaphore_signal(barrier, inc=1, device_id={"cols": p}, device_id_type=MESH)
    for p in row_peers:
        pl.semaphore_signal(barrier, inc=1, device_id={"rows": p}, device_id_type=MESH)

    fetches = [pltpu.make_async_copy(src, dst, in_sem.at[n])
               for n, (src, dst) in enumerate(((a_hbm, a_in), (b_hbm, b_in), (c_hbm, c_in)))]
    for fetch in fetches:
        fetch.start()

    sides = (near, 1 - near)
    for side in range(2):
        for d in range(nr):
            for s in range(per):
                load(sides[side], chunk(side, d) * per + s).start()

    for fetch in fetches:
        fetch.wait()
    all_a[0, col] = a_in[...].astype(BF16)
    all_b[0, row] = b_in[...].astype(BF16)

    pl.semaphore_wait(barrier, nc + nr - 2)

    class Exchange:
        def __init__(self, send, recv, ss, rs, axis, me):
            self.args = (send, recv, ss, rs, axis, me)

        def to(self, p):
            send, recv, ss, rs, axis, me = self.args
            return pltpu.make_async_remote_copy(
                src_ref=recv.at[me] if send is None else send.at[p], dst_ref=recv.at[me],
                send_sem=ss.at[p], recv_sem=rs.at[me], device_id={axis: p}, device_id_type=MESH)

        def start(self, peers):
            for p in peers:
                self.to(p).start()

        def wait_recv(self, peers):
            send, recv, ss, rs, axis, me = self.args
            for p in peers:
                pltpu.make_async_remote_copy(
                    src_ref=recv.at[p], dst_ref=recv.at[p], send_sem=ss.at[p], recv_sem=rs.at[p],
                    device_id={axis: p}, device_id_type=MESH).wait_recv()

        def wait_send(self, peers):
            for p in peers:
                self.to(p).wait_send()

    pending = []
    local_a, local_b, shared_c = a_in[...], b_in[...], c_in[...]

    def gather(it):
        return (Exchange(None, all_a.at[it], ag_send.at[it], ag_recv.at[it], "cols", col),
                Exchange(None, all_b.at[it], bg_send.at[it], bg_recv.at[it], "rows", row))

    gather_a, gather_b = gather(0)
    gather_b.start(row_peers)
    gather_a.start(col_peers)

    for it in range(ITERS):
        pending += [(gather_a, col_peers), (gather_b, row_peers)]
        scatter_a = Exchange(send_a.at[it], recv_a.at[it], ar_send.at[it], ar_recv.at[it], "cols", col)
        scatter_b = Exchange(send_b.at[it], recv_b.at[it], br_send.at[it], br_recv.at[it], "rows", row)
        cols_c = Exchange(None, part_c.at[it], c1_send.at[it], c1_recv.at[it], "cols", col)
        rows_c = Exchange(None, sum_c.at[it], c2_send.at[it], c2_recv.at[it], "rows", row)
        pending += [(scatter_a, col_peers), (scatter_b, row_peers), (cols_c, col_peers), (rows_c, row_peers)]
        acc_a[...] = jnp.zeros_like(acc_a)
        acc_c[...] = jnp.zeros_like(acc_c)

        for side in range(2):
            h = sides[side]
            gather_a.wait_recv((near_peers, far_peers)[side])
            rows_a = all_a[it, pl.ds(h * half, half)].reshape(half_rows, rank)
            held_a[...] = rows_a
            trans_a[...] = rows_a.T

            def produce(q, s, slot):
                t = q * per + s
                if side == 0:
                    rows_b = all_b[it, q, pl.ds(s * width, width), :].astype(F32)
                    scaled[t] = (rows_b[:, None, :] * shared_c[None, :, :]).astype(BF16).reshape(tile, rank)
                log_rate = lax.dot_general(
                    held_a[...], scaled[t], (((1,), (1,)), ((), ())), preferred_element_type=F32)
                resid[slot] = (jnp.exp(log_rate) - counts[h, t].astype(F32)).astype(BF16)

            def consume(q, s, slot):
                t = q * per + s
                acc_a[h] += jnp.dot(resid[slot], scaled[t], preferred_element_type=F32)
                turned = jnp.dot(trans_a[...], resid[slot], preferred_element_type=F32)
                if side == 0:
                    mixed_t[t] = turned
                    return
                mixed = (mixed_t[t] + turned).T.reshape(width, depth, rank)
                rows_b = all_b[it, q, pl.ds(s * width, width), :].astype(F32)
                grad_b[pl.ds(s * width, width), :] = jnp.sum(mixed * shared_c[None, :, :], axis=1)
                acc_c[...] += jnp.sum(mixed * rows_b[:, None, :], axis=0)

            def ready(d):
                q = chunk(side, d)
                if it == 0:
                    for s in range(per):
                        load(h, q * per + s).wait()
                return q

            def step(d, carry):
                q, q_next = chunk(side, d), chunk(side, d + 1)
                if side == 0 or it == 0:
                    @pl.when(d < nr - 1)
                    def _():
                        ready(d + 1)
                        if side == 0:
                            gather_b.wait_recv([q_next])
                for s in range(per):
                    if s + 1 < per:
                        produce(q, s + 1, (s + 1) % 2)
                    else:
                        produce(q_next, 0, 0)
                    consume(q, s, s % 2)
                if side == 1:
                    send_b[it, q] = grad_b[...].astype(BF16)

                    @pl.when(d < nr - 1)
                    def _():
                        scatter_b.start([q])

                return carry

            produce(ready(0), 0, 0)
            lax.fori_loop(0, nr, step, 0)

            if side == 1:
                part_c[it, col] = acc_c[...].astype(BF16)
                cols_c.start(far_peers + near_peers)
            for k in range(half):
                send_a[it, h * half + k] = acc_a[h, pl.ds(k * own_a, own_a), :].astype(BF16)
            scatter_a.start((near_peers, far_peers)[side])

        last = it == ITERS - 1
        if not last:
            gather_a, gather_b = gather(it + 1)

        scatter_b.wait_recv(row_peers)
        recv_b[it, row] = jnp.zeros((own_b, rank), BF16)
        total_b = grad_b[...] + jnp.sum(recv_b[it].astype(F32), axis=0)
        local_b = local_b - rate_b * total_b
        if last:
            b_out[...] = local_b
        else:
            all_b[it + 1, row] = local_b.astype(BF16)
            gather_b.start(row_peers)

        cols_c.wait_recv(col_peers)
        sum_c[it, row] = jnp.sum(part_c[it].astype(F32), axis=0)
        rows_c.start(row_peers)

        scatter_a.wait_recv(col_peers)
        recv_a[it, col] = jnp.zeros((own_a, rank), BF16)
        total_a = acc_a[near, pl.ds(pl.multiple_of(spot * own_a, own_a), own_a), :] + jnp.sum(recv_a[it].astype(F32), axis=0)
        local_a = local_a - rate_a * total_a
        if last:
            a_out[...] = local_a
        else:
            all_a[it + 1, col] = local_a.astype(BF16)
            gather_a.start(col_peers)

        rows_c.wait_recv(row_peers)
        shared_c = shared_c - rate_c * jnp.sum(sum_c[it], axis=0)
        if last:
            c_out[...] = shared_c

    for group, peers in pending:
        group.wait_send(peers)


def finish(a, b, c, a_out, b_out, c_out):
    a_out[...] = a[...]
    b_out[...] = b[...]
    c_out[...] = c[...]


def local(nr, nc, counts, start_a, start_b, start_c):
    rows_here, flat_width = counts.shape
    own_a, rank = start_a.shape
    own_b = start_b.shape[0]
    depth = start_c.shape[0]
    cols_here = flat_width // depth
    total_i, total_j = rows_here * nr, cols_here * nc
    rates = (0.3 / math.sqrt(total_j * depth), 0.3 / math.sqrt(total_i * depth), 0.3 / math.sqrt(total_i * total_j))
    tile = 512
    tiles = flat_width // tile
    vmem = pl.BlockSpec(memory_space=pltpu.VMEM)
    dma = pltpu.SemaphoreType.DMA
    outs = [jax.ShapeDtypeStruct(x.shape, F32) for x in (start_a, start_b, start_c)]
    half_rows = rows_here // 2
    found = pl.pallas_call(
        functools.partial(kernel, nr, nc, tile, rates),
        out_shape=[pltpu.VMEM(x.shape, F32) for x in (start_a, start_b, start_c)],
        in_specs=[pl.BlockSpec(memory_space=pl.ANY)] * 4,
        out_specs=[vmem] * 3,
        scratch_shapes=[
            pltpu.VMEM(start_a.shape, F32), pltpu.VMEM(start_b.shape, F32), pltpu.VMEM(start_c.shape, F32),
            dma((3,)),
            pltpu.VMEM((2, tiles, half_rows, tile), BF16),
            pltpu.VMEM((ITERS, nc, own_a, rank), BF16),
            pltpu.VMEM((ITERS, nr, own_b, rank), BF16),
            pltpu.VMEM((ITERS, nc, own_a, rank), BF16),
            pltpu.VMEM((ITERS, nr, own_b, rank), BF16),
            pltpu.VMEM((ITERS, nc, own_a, rank), BF16),
            pltpu.VMEM((ITERS, nr, own_b, rank), BF16),
            pltpu.VMEM((ITERS, nc, depth, rank), BF16),
            pltpu.VMEM((ITERS, nr, depth, rank), F32),
            pltpu.VMEM((half_rows, rank), BF16),
            pltpu.VMEM((rank, half_rows), BF16),
            pltpu.VMEM((2, half_rows, rank), F32),
            pltpu.VMEM((depth, rank), F32),
            pltpu.VMEM((2, half_rows, tile), BF16),
            pltpu.VMEM((tiles, tile, rank), BF16),
            pltpu.VMEM((tiles, rank, tile), F32),
            pltpu.VMEM((own_b, rank), F32),
            dma((2, tiles)),
            dma((ITERS, nc)), dma((ITERS, nc)), dma((ITERS, nr)), dma((ITERS, nr)),
            dma((ITERS, nc)), dma((ITERS, nc)), dma((ITERS, nr)), dma((ITERS, nr)),
            dma((ITERS, nc)), dma((ITERS, nc)), dma((ITERS, nr)), dma((ITERS, nr)),
        ],
        compiler_params=pltpu.CompilerParams(
            collective_id=0, has_side_effects=True, vmem_limit_bytes=56 * 1024 * 1024),
    )(counts, start_a, start_b, start_c)
    held = [pltpu.with_memory_space_constraint(x, pltpu.VMEM) for x in found]
    return pl.pallas_call(finish, out_shape=outs, in_specs=[vmem] * 3, out_specs=[vmem] * 3)(*held)


def solution(mesh):
    nr, nc = mesh.shape["rows"], mesh.shape["cols"]
    placed = (P("rows", "cols"), P(("rows", "cols"), None), P(("cols", "rows"), None), P())
    return jax.shard_map(
        functools.partial(local, nr, nc),
        mesh=mesh,
        in_specs=placed,
        out_specs=(P(("rows", "cols"), None), P(("cols", "rows"), None), P()),
        check_vma=False,
    )
```

```python
import functools
import math

import jax
import jax.numpy as jnp
from jax import lax
from jax.experimental import pallas as pl
from jax.experimental.pallas import tpu as pltpu
from jax.sharding import PartitionSpec as P

ITERS = 2
LATE = 0
MESH = pl.DeviceIdType.MESH
F32 = jnp.float32
BF16 = jnp.bfloat16


def kernel(nr, nc, tile, rates, counts_hbm, a_hbm, b_hbm, c_hbm, a_out, b_out, c_out,
           a_now, b_now, c_in, in_sem, counts, all_a, all_b, send_a, send_b, recv_a, recv_b, part_c, sum_c,
           held_a, trans_a, acc_a, acc_c, resid, resid_late, scaled, mixed_t, grad_b,
           cnt_sem, ag_send, ag_recv, bg_send, bg_recv, ar_send, ar_recv, br_send, br_recv,
           c1_send, c1_recv, c2_send, c2_recv):
    row, col = lax.axis_index("rows"), lax.axis_index("cols")
    rate_a, rate_b, rate_c = rates
    own_a, rank = a_now.shape
    own_b = b_now.shape[0]
    depth = c_in.shape[0]
    tiles = counts.shape[1]
    per = tiles // nr
    width = tile // depth

    half, quarter = nc // 2, nc // 4
    seat = lax.rem(col + nc - quarter, nc)
    mine, spot = lax.div(seat, half), lax.rem(seat, half)
    col_peers = [lax.rem(seat + off, nc) for off in range(1, nc)]
    row_peers = [lax.rem(row + off, nr) for off in range(1, nr)]
    half_rows = half * own_a
    quarter_rows = quarter * own_a

    def at_col(p):
        return {"cols": lax.rem(p + quarter, nc)}

    def at_row(p):
        return {"rows": p}

    barrier = pltpu.get_barrier_semaphore()
    for p in col_peers:
        pl.semaphore_signal(barrier, inc=1, device_id=at_col(p), device_id_type=MESH)
    for p in row_peers:
        pl.semaphore_signal(barrier, inc=1, device_id=at_row(p), device_id_type=MESH)

    fetches = [pltpu.make_async_copy(src, dst, in_sem.at[n])
               for n, (src, dst) in enumerate(((a_hbm, a_now), (b_hbm, b_now), (c_hbm, c_in)))]
    for fetch in fetches:
        fetch.start()

    def loads(h, t):
        spans = [(quarter_rows, half_rows, 0)] if h == 0 else [(3 * quarter_rows, quarter_rows, 0), (0, quarter_rows, quarter_rows)]
        return [pltpu.make_async_copy(
            counts_hbm.at[pl.ds(first, n), pl.ds(pl.multiple_of(t * tile, tile), tile)],
            counts.at[h, t, pl.ds(to, n)], cnt_sem.at[h + k, t]) for k, (first, n, to) in enumerate(spans)]

    def chunk(side, d):
        return lax.rem(row + side + d, nr)

    for fetch in fetches:
        fetch.wait()
    all_a[0, seat] = a_now[...].astype(BF16)
    all_b[0, row] = b_now[...].astype(BF16)

    pl.semaphore_wait(barrier, nc + nr - 2)

    class Exchange:
        def __init__(self, send, recv, ss, rs, at, me):
            self.args = (send, recv, ss, rs, at, me)

        def to(self, p):
            send, recv, ss, rs, at, me = self.args
            return pltpu.make_async_remote_copy(
                src_ref=recv.at[me] if send is None else send.at[p], dst_ref=recv.at[me],
                send_sem=ss.at[p], recv_sem=rs.at[me], device_id=at(p), device_id_type=MESH)

        def start(self, peers):
            for p in peers:
                self.to(p).start()

        def wait_recv(self, peers):
            send, recv, ss, rs, at, me = self.args
            for p in peers:
                pltpu.make_async_remote_copy(
                    src_ref=recv.at[p], dst_ref=recv.at[p], send_sem=ss.at[p], recv_sem=rs.at[p],
                    device_id=at(p), device_id_type=MESH).wait_recv()

        def wait_send(self, peers):
            for p in peers:
                self.to(p).wait_send()

    def over_half(act, h):
        act([h * half + lax.rem(spot + off, half) for off in range(1, half)])

        @pl.when(mine != h)
        def _():
            act([h * half + spot])

    pending = []
    shared_c = c_in[...]

    def gather(it):
        return (Exchange(None, all_a.at[it], ag_send.at[it], ag_recv.at[it], at_col, seat),
                Exchange(None, all_b.at[it], bg_send.at[it], bg_recv.at[it], at_row, row))

    gather_a, gather_b = gather(0)
    gather_b.start(row_peers)
    gather_a.start(col_peers)
    for h in range(2):
        for d in range(nr):
            for s in range(per):
                for load in loads(h, chunk(h, d) * per + s):
                    load.start()

    late_update = None

    for it in range(ITERS):
        last = it == ITERS - 1
        pending += [(gather_a, col_peers), (gather_b, row_peers)]
        scatter_a = Exchange(send_a.at[it], recv_a.at[it], ar_send.at[it], ar_recv.at[it], at_col, seat)
        scatter_b = Exchange(send_b.at[it], recv_b.at[it], br_send.at[it], br_recv.at[it], at_row, row)
        cols_c = Exchange(None, part_c.at[it], c1_send.at[it], c1_recv.at[it], at_col, seat)
        rows_c = Exchange(None, sum_c.at[it], c2_send.at[it], c2_recv.at[it], at_row, row)
        pending += [(scatter_a, col_peers), (scatter_b, row_peers), (cols_c, col_peers), (rows_c, row_peers)]
        if not last:
            next_a, next_b = gather(it + 1)
        acc_c[...] = jnp.zeros_like(acc_c)

        def send_half(h, it=it, scatter_a=scatter_a):
            for k in range(half):
                send_a[it, h * half + k] = acc_a[h, pl.ds(k * own_a, own_a), :].astype(BF16)
            over_half(scatter_a.start, h)

        def update_a(it=it, last=last, scatter_a=scatter_a, next_a=None if last else next_a):
            scatter_a.wait_recv(col_peers)
            recv_a[it, seat] = jnp.zeros((own_a, rank), BF16)
            total = (acc_a[mine, pl.ds(pl.multiple_of(spot * own_a, own_a), own_a), :]
                     + jnp.sum(recv_a[it].astype(F32), axis=0))
            if last:
                a_out[...] = a_now[...] - rate_a * total
            else:
                a_now[...] = a_now[...] - rate_a * total
                all_a[it + 1, seat] = a_now[...].astype(BF16)
                next_a.start(col_peers)

        for h in range(2):
            over_half(gather_a.wait_recv, h)
            rows_a = all_a[it, pl.ds(h * half, half)].reshape(half_rows, rank)
            held_a[...] = rows_a
            trans_a[...] = rows_a.T
            if h == 0:
                acc_a[0] = jnp.zeros((half_rows, rank), F32)

            def produce(q, s, slot):
                t = q * per + s
                if h == 0:
                    rows_b = all_b[it, q, pl.ds(s * width, width), :].astype(F32)
                    scaled[t] = (rows_b[:, None, :] * shared_c[None, :, :]).astype(BF16).reshape(tile, rank)
                log_rate = lax.dot_general(
                    held_a[...], scaled[t], (((1,), (1,)), ((), ())), preferred_element_type=F32)
                found = (jnp.exp(log_rate) - counts[h, t].astype(F32)).astype(BF16)
                if h == 0:
                    resid[slot] = found
                else:
                    resid_late[t] = found

            def consume(q, s, slot):
                t = q * per + s
                if h == 0:
                    acc_a[0] += jnp.dot(resid[slot], scaled[t], preferred_element_type=F32)
                    mixed_t[t] = jnp.dot(trans_a[...], resid[slot], preferred_element_type=F32)
                    return
                turned = jnp.dot(trans_a[...], resid_late[t], preferred_element_type=F32)
                mixed = (mixed_t[t] + turned).T.reshape(width, depth, rank)
                rows_b = all_b[it, q, pl.ds(s * width, width), :].astype(F32)
                grad_b[pl.ds(s * width, width), :] = jnp.sum(mixed * shared_c[None, :, :], axis=1)
                acc_c[...] += jnp.sum(mixed * rows_b[:, None, :], axis=0)

            def ready(d):
                q = chunk(h, d)
                if it == 0:
                    for s in range(per):
                        for load in loads(h, q * per + s):
                            load.wait()
                return q

            def step(d, carry):
                q, q_next = chunk(h, d), chunk(h, d + 1)
                if h == 0 or it == 0:
                    @pl.when(d < nr - 1)
                    def _():
                        ready(d + 1)
                        if h == 0:
                            gather_b.wait_recv([q_next])
                for s in range(per):
                    if s + 1 < per:
                        produce(q, s + 1, (s + 1) % 2)
                    else:
                        produce(q_next, 0, 0)
                    consume(q, s, s % 2)
                if h == 0 and late_update is not None:
                    @pl.when((d == LATE) & (mine == 1))
                    def _():
                        late_update()
                if h == 1:
                    send_b[it, q] = grad_b[...].astype(BF16)

                    @pl.when(d < nr - 1)
                    def _():
                        scatter_b.start([q])

                return carry

            produce(ready(0), 0, 0)
            lax.fori_loop(0, nr, step, 0)
            if h == 0:
                send_half(0)

        part_c[it, seat] = acc_c[...].astype(BF16)
        cols_c.start(col_peers)

        acc_a[1] = jnp.zeros((half_rows, rank), F32)

        def gather_grad(g, carry):
            total = acc_a[1]
            for s in range(per):
                total += jnp.dot(resid_late[g * per + s], scaled[g * per + s], preferred_element_type=F32)
            acc_a[1] = total
            return carry

        lax.fori_loop(0, nr, gather_grad, 0)
        send_half(1)

        scatter_b.wait_recv(row_peers)
        recv_b[it, row] = jnp.zeros((own_b, rank), BF16)
        b_next = b_now[...] - rate_b * (grad_b[...] + jnp.sum(recv_b[it].astype(F32), axis=0))
        if last:
            b_out[...] = b_next
        else:
            b_now[...] = b_next
            all_b[it + 1, row] = b_next.astype(BF16)
            next_b.start(row_peers)

        @pl.when(mine == 0)
        def _():
            update_a()

        cols_c.wait_recv(col_peers)
        sum_c[it, row] = jnp.sum(part_c[it].astype(F32), axis=0)
        rows_c.start(row_peers)

        if last:
            @pl.when(mine == 1)
            def _():
                update_a()
        late_update = update_a

        rows_c.wait_recv(row_peers)
        shared_c = shared_c - rate_c * jnp.sum(sum_c[it], axis=0)
        if last:
            c_out[...] = shared_c
        else:
            gather_a, gather_b = next_a, next_b

    for group, peers in pending:
        group.wait_send(peers)


def finish(a, b, c, a_out, b_out, c_out):
    a_out[...] = a[...]
    b_out[...] = b[...]
    c_out[...] = c[...]


def local(nr, nc, counts, start_a, start_b, start_c):
    rows_here, flat_width = counts.shape
    own_a, rank = start_a.shape
    own_b = start_b.shape[0]
    depth = start_c.shape[0]
    cols_here = flat_width // depth
    total_i, total_j = rows_here * nr, cols_here * nc
    rates = (0.3 / math.sqrt(total_j * depth), 0.3 / math.sqrt(total_i * depth), 0.3 / math.sqrt(total_i * total_j))
    tile = 512
    tiles = flat_width // tile
    vmem = pl.BlockSpec(memory_space=pltpu.VMEM)
    dma = pltpu.SemaphoreType.DMA
    outs = [jax.ShapeDtypeStruct(x.shape, F32) for x in (start_a, start_b, start_c)]
    half_rows = rows_here // 2
    found = pl.pallas_call(
        functools.partial(kernel, nr, nc, tile, rates),
        out_shape=[pltpu.VMEM(x.shape, F32) for x in (start_a, start_b, start_c)],
        in_specs=[pl.BlockSpec(memory_space=pl.ANY)] * 4,
        out_specs=[vmem] * 3,
        scratch_shapes=[
            pltpu.VMEM(start_a.shape, F32), pltpu.VMEM(start_b.shape, F32), pltpu.VMEM(start_c.shape, F32),
            dma((3,)),
            pltpu.VMEM((2, tiles, half_rows, tile), BF16),
            pltpu.VMEM((ITERS, nc, own_a, rank), BF16),
            pltpu.VMEM((ITERS, nr, own_b, rank), BF16),
            pltpu.VMEM((ITERS, nc, own_a, rank), BF16),
            pltpu.VMEM((ITERS, nr, own_b, rank), BF16),
            pltpu.VMEM((ITERS, nc, own_a, rank), BF16),
            pltpu.VMEM((ITERS, nr, own_b, rank), BF16),
            pltpu.VMEM((ITERS, nc, depth, rank), BF16),
            pltpu.VMEM((ITERS, nr, depth, rank), F32),
            pltpu.VMEM((half_rows, rank), BF16),
            pltpu.VMEM((rank, half_rows), BF16),
            pltpu.VMEM((2, half_rows, rank), F32),
            pltpu.VMEM((depth, rank), F32),
            pltpu.VMEM((2, half_rows, tile), BF16),
            pltpu.VMEM((tiles, half_rows, tile), BF16),
            pltpu.VMEM((tiles, tile, rank), BF16),
            pltpu.VMEM((tiles, rank, tile), F32),
            pltpu.VMEM((own_b, rank), F32),
            dma((3, tiles)),
            dma((ITERS, nc)), dma((ITERS, nc)), dma((ITERS, nr)), dma((ITERS, nr)),
            dma((ITERS, nc)), dma((ITERS, nc)), dma((ITERS, nr)), dma((ITERS, nr)),
            dma((ITERS, nc)), dma((ITERS, nc)), dma((ITERS, nr)), dma((ITERS, nr)),
        ],
        compiler_params=pltpu.CompilerParams(
            collective_id=0, has_side_effects=True, vmem_limit_bytes=56 * 1024 * 1024),
    )(counts, start_a, start_b, start_c)
    held = [pltpu.with_memory_space_constraint(x, pltpu.VMEM) for x in found]
    return pl.pallas_call(finish, out_shape=outs, in_specs=[vmem] * 3, out_specs=[vmem] * 3)(*held)


def solution(mesh):
    nr, nc = mesh.shape["rows"], mesh.shape["cols"]
    placed = (P("rows", "cols"), P(("rows", "cols"), None), P(("cols", "rows"), None), P())
    return jax.shard_map(
        functools.partial(local, nr, nc),
        mesh=mesh,
        in_specs=placed,
        out_specs=(P(("rows", "cols"), None), P(("cols", "rows"), None), P()),
        check_vma=False,
    )
```

```python
import functools
import math

import jax
import jax.numpy as jnp
from jax import lax
from jax.experimental import pallas as pl
from jax.experimental.pallas import tpu as pltpu
from jax.sharding import PartitionSpec as P

ITERS = 2
MESH = pl.DeviceIdType.MESH
F32 = jnp.float32
BF16 = jnp.bfloat16


def kernel(nr, nc, tile, rates, counts_hbm, a_hbm, b_hbm, c_hbm, a_out, b_out, c_out,
           a_now, b_now, c_in, in_sem, counts, all_a, all_b, send_a, send_b, recv_a, recv_b, part_c, sum_c,
           held_a, trans_a, acc_a, acc_c, resid, scaled, mixed_t, grad_b,
           cnt_sem, ag_send, ag_recv, bg_send, bg_recv, ar_send, ar_recv, br_send, br_recv,
           c1_send, c1_recv, c2_send, c2_recv):
    row, col = lax.axis_index("rows"), lax.axis_index("cols")
    rate_a, rate_b, rate_c = rates
    own_a, rank = a_now.shape
    own_b = b_now.shape[0]
    depth = c_in.shape[0]
    tiles = scaled.shape[0]
    per = tiles // nr
    span = per * tile
    width = tile // depth

    half, quarter = nc // 2, nc // 4
    seat = lax.rem(col + nc - quarter, nc)
    mine, spot = lax.div(seat, half), lax.rem(seat, half)
    col_peers = [lax.rem(seat + off, nc) for off in range(1, nc)]
    row_peers = [lax.rem(row + off, nr) for off in range(1, nr)]
    half_rows = half * own_a
    quarter_rows = quarter * own_a

    def at_col(p):
        return {"cols": lax.rem(p + quarter, nc)}

    def at_row(p):
        return {"rows": p}

    barrier = pltpu.get_barrier_semaphore()
    for p in col_peers:
        pl.semaphore_signal(barrier, inc=1, device_id=at_col(p), device_id_type=MESH)
    for p in row_peers:
        pl.semaphore_signal(barrier, inc=1, device_id=at_row(p), device_id_type=MESH)

    fetches = [pltpu.make_async_copy(src, dst, in_sem.at[n])
               for n, (src, dst) in enumerate(((a_hbm, a_now), (b_hbm, b_now), (c_hbm, c_in)))]
    for fetch in fetches:
        fetch.start()

    def loads(h, q):
        spans = [(quarter_rows, half_rows, 0)] if h == 0 else [(3 * quarter_rows, quarter_rows, 0), (0, quarter_rows, quarter_rows)]
        return [pltpu.make_async_copy(
            counts_hbm.at[pl.ds(first, n), pl.ds(pl.multiple_of(q * span, span), span)],
            counts.at[h, q, pl.ds(to, n)], cnt_sem.at[h + k, q]) for k, (first, n, to) in enumerate(spans)]

    def chunk(side, d):
        return lax.rem(row + side + d, nr)

    for fetch in fetches:
        fetch.wait()
    all_a[0, seat] = a_now[...].astype(BF16)
    all_b[0, row] = b_now[...].astype(BF16)

    pl.semaphore_wait(barrier, nc + nr - 2)

    class Exchange:
        def __init__(self, send, recv, ss, rs, at, me, group):
            self.args = (send, recv, ss, rs, at, me)
            self.group = group

        def to(self, p):
            send, recv, ss, rs, at, me = self.args
            return pltpu.make_async_remote_copy(
                src_ref=recv.at[me] if send is None else send.at[p], dst_ref=recv.at[me],
                send_sem=ss, recv_sem=self.seat_sem(me), device_id=at(p), device_id_type=MESH)

        def start(self, peers):
            for p in peers:
                self.to(p).start()

        def seat_sem(self, p):
            rs, group = self.args[3], self.group
            return rs.at[lax.div(p, group)]

        def bytes_of(self, n, p):
            send, recv, ss, rs, at, me = self.args
            return pltpu.make_async_remote_copy(
                src_ref=recv.at[pl.ds(0, n)], dst_ref=recv.at[pl.ds(0, n)], send_sem=ss, recv_sem=self.seat_sem(p),
                device_id=at(lax.rem(me + 1, recv.shape[0])), device_id_type=MESH)

        def wait_recv(self, n, p):
            self.bytes_of(n, p).wait_recv()

        def wait_send(self):
            self.bytes_of(self.args[1].shape[0] - 1, self.args[5]).wait_send()

    def over_half(act, h):
        act([h * half + lax.rem(spot + off, half) for off in range(1, half)])

        @pl.when(mine != h)
        def _():
            act([h * half + spot])

    pending = []
    shared_c = c_in[...]

    def gather(it):
        return (Exchange(None, all_a.at[it], ag_send.at[it], ag_recv.at[it], at_col, seat, half),
                Exchange(None, all_b.at[it], bg_send.at[it], bg_recv.at[it], at_row, row, 1))

    gather_a, gather_b = gather(0)
    gather_b.start(row_peers)
    gather_a.start(col_peers)
    for h in range(2):
        for d in range(nr):
            for load in loads(h, chunk(h, d)):
                load.start()

    for it in range(ITERS):
        last = it == ITERS - 1
        pending += [gather_a, gather_b]
        scatter_a = Exchange(send_a.at[it], recv_a.at[it], ar_send.at[it], ar_recv.at[it], at_col, seat, nc)
        scatter_b = Exchange(send_b.at[it], recv_b.at[it], br_send.at[it], br_recv.at[it], at_row, row, nr)
        cols_c = Exchange(None, part_c.at[it], c1_send.at[it], c1_recv.at[it], at_col, seat, nc)
        rows_c = Exchange(None, sum_c.at[it], c2_send.at[it], c2_recv.at[it], at_row, row, nr)
        pending += [scatter_a, scatter_b, cols_c, rows_c]
        if not last:
            next_a, next_b = gather(it + 1)
        acc_c[...] = jnp.zeros_like(acc_c)

        def send_half(h, it=it, scatter_a=scatter_a):
            for k in range(half):
                send_a[it, h * half + k] = acc_a[h, pl.ds(k * own_a, own_a), :].astype(BF16)
            over_half(scatter_a.start, h)

        def update_a(it=it, last=last, scatter_a=scatter_a, next_a=None if last else next_a):
            scatter_a.wait_recv(nc - 1, 0)
            recv_a[it, seat] = jnp.zeros((own_a, rank), BF16)
            total = (acc_a[mine, pl.ds(pl.multiple_of(spot * own_a, own_a), own_a), :]
                     + jnp.sum(recv_a[it].astype(F32), axis=0))
            if last:
                a_out[...] = a_now[...] - rate_a * total
            else:
                a_now[...] = a_now[...] - rate_a * total
                all_a[it + 1, seat] = a_now[...].astype(BF16)
                next_a.start(col_peers)

        for h in range(2):
            @pl.when(mine == h)
            def _():
                gather_a.wait_recv(half - 1, h * half)

            @pl.when(mine != h)
            def _():
                gather_a.wait_recv(half, h * half)

            rows_a = all_a[it, pl.ds(h * half, half)].reshape(half_rows, rank)
            held_a[...] = rows_a
            trans_a[...] = rows_a.T
            acc_a[h] = jnp.zeros((half_rows, rank), F32)

            def produce(q, s, slot):
                t = q * per + s
                if h == 0:
                    rows_b = all_b[it, q, pl.ds(s * width, width), :].astype(F32)
                    scaled[t] = (rows_b[:, None, :] * shared_c[None, :, :]).astype(BF16).reshape(tile, rank)
                log_rate = lax.dot_general(
                    held_a[...], scaled[t], (((1,), (1,)), ((), ())), preferred_element_type=F32)
                resid[slot] = (jnp.exp(log_rate) - counts[h, q, :, pl.ds(s * tile, tile)].astype(F32)).astype(BF16)

            def consume(q, s, slot):
                t = q * per + s
                acc_a[h] += jnp.dot(resid[slot], scaled[t], preferred_element_type=F32)
                turned = jnp.dot(trans_a[...], resid[slot], preferred_element_type=F32)
                if h == 0:
                    mixed_t[t] = turned
                    return
                mixed = (mixed_t[t] + turned).T.reshape(width, depth, rank)
                rows_b = all_b[it, q, pl.ds(s * width, width), :].astype(F32)
                grad_b[pl.ds(s * width, width), :] = jnp.sum(mixed * shared_c[None, :, :], axis=1)
                acc_c[...] += jnp.sum(mixed * rows_b[:, None, :], axis=0)

            def ready(d):
                q = chunk(h, d)
                if it == 0:
                    for load in loads(h, q):
                        load.wait()
                return q

            def step(d, carry):
                q, q_next = chunk(h, d), chunk(h, d + 1)
                if h == 0 or it == 0:
                    @pl.when(d < nr - 1)
                    def _():
                        ready(d + 1)
                        if h == 0:
                            gather_b.wait_recv(1, q_next)
                for s in range(per):
                    if s + 1 < per:
                        produce(q, s + 1, (s + 1) % 2)
                    else:
                        produce(q_next, 0, 0)
                    consume(q, s, s % 2)
                if h == 1:
                    send_b[it, q] = grad_b[...].astype(BF16)

                    @pl.when(d < nr - 1)
                    def _():
                        scatter_b.start([q])

                return carry

            produce(ready(0), 0, 0)
            lax.fori_loop(0, nr, step, 0)
            if h == 0:
                send_half(0)

        part_c[it, seat] = acc_c[...].astype(BF16)
        cols_c.start(col_peers)

        send_half(1)

        scatter_b.wait_recv(nr - 1, 0)
        recv_b[it, row] = jnp.zeros((own_b, rank), BF16)
        b_next = b_now[...] - rate_b * (grad_b[...] + jnp.sum(recv_b[it].astype(F32), axis=0))
        if last:
            b_out[...] = b_next
        else:
            b_now[...] = b_next
            all_b[it + 1, row] = b_next.astype(BF16)
            next_b.start(row_peers)

        @pl.when(mine == 0)
        def _():
            update_a()

        cols_c.wait_recv(nc - 1, 0)
        sum_c[it, row] = jnp.sum(part_c[it].astype(F32), axis=0)
        rows_c.start(row_peers)

        if last:
            @pl.when(mine == 1)
            def _():
                update_a()
        rows_c.wait_recv(nr - 1, 0)
        shared_c = shared_c - rate_c * jnp.sum(sum_c[it], axis=0)
        if last:
            c_out[...] = shared_c
        else:
            @pl.when(mine == 1)
            def _():
                update_a()
            gather_a, gather_b = next_a, next_b

    for group in pending:
        group.wait_send()


def finish(a, b, c, a_out, b_out, c_out):
    a_out[...] = a[...]
    b_out[...] = b[...]
    c_out[...] = c[...]


def local(nr, nc, counts, start_a, start_b, start_c):
    rows_here, flat_width = counts.shape
    own_a, rank = start_a.shape
    own_b = start_b.shape[0]
    depth = start_c.shape[0]
    cols_here = flat_width // depth
    total_i, total_j = rows_here * nr, cols_here * nc
    rates = (0.3 / math.sqrt(total_j * depth), 0.3 / math.sqrt(total_i * depth), 0.3 / math.sqrt(total_i * total_j))
    tile = 512
    tiles = flat_width // tile
    vmem = pl.BlockSpec(memory_space=pltpu.VMEM)
    dma = pltpu.SemaphoreType.DMA
    outs = [jax.ShapeDtypeStruct(x.shape, F32) for x in (start_a, start_b, start_c)]
    half_rows = rows_here // 2
    found = pl.pallas_call(
        functools.partial(kernel, nr, nc, tile, rates),
        out_shape=[pltpu.VMEM(x.shape, F32) for x in (start_a, start_b, start_c)],
        in_specs=[pl.BlockSpec(memory_space=pl.ANY)] * 4,
        out_specs=[vmem] * 3,
        scratch_shapes=[
            pltpu.VMEM(start_a.shape, F32), pltpu.VMEM(start_b.shape, F32), pltpu.VMEM(start_c.shape, F32),
            dma((3,)),
            pltpu.VMEM((2, nr, half_rows, flat_width // nr), BF16),
            pltpu.VMEM((ITERS, nc, own_a, rank), BF16),
            pltpu.VMEM((ITERS, nr, own_b, rank), BF16),
            pltpu.VMEM((ITERS, nc, own_a, rank), BF16),
            pltpu.VMEM((ITERS, nr, own_b, rank), BF16),
            pltpu.VMEM((ITERS, nc, own_a, rank), BF16),
            pltpu.VMEM((ITERS, nr, own_b, rank), BF16),
            pltpu.VMEM((ITERS, nc, depth, rank), BF16),
            pltpu.VMEM((ITERS, nr, depth, rank), F32),
            pltpu.VMEM((half_rows, rank), BF16),
            pltpu.VMEM((rank, half_rows), BF16),
            pltpu.VMEM((2, half_rows, rank), F32),
            pltpu.VMEM((depth, rank), F32),
            pltpu.VMEM((2, half_rows, tile), BF16),
            pltpu.VMEM((tiles, tile, rank), BF16),
            pltpu.VMEM((tiles, rank, tile), F32),
            pltpu.VMEM((own_b, rank), F32),
            dma((3, nr)),
            dma((ITERS,)), dma((ITERS, 2)), dma((ITERS,)), dma((ITERS, nr)),
            dma((ITERS,)), dma((ITERS, 1)), dma((ITERS,)), dma((ITERS, 1)),
            dma((ITERS,)), dma((ITERS, 1)), dma((ITERS,)), dma((ITERS, 1)),
        ],
        compiler_params=pltpu.CompilerParams(
            collective_id=0, has_side_effects=True, vmem_limit_bytes=56 * 1024 * 1024),
    )(counts, start_a, start_b, start_c)
    held = [pltpu.with_memory_space_constraint(x, pltpu.VMEM) for x in found]
    return pl.pallas_call(finish, out_shape=outs, in_specs=[vmem] * 3, out_specs=[vmem] * 3)(*held)


def solution(mesh):
    nr, nc = mesh.shape["rows"], mesh.shape["cols"]
    placed = (P("rows", "cols"), P(("rows", "cols"), None), P(("cols", "rows"), None), P())
    return jax.shard_map(
        functools.partial(local, nr, nc),
        mesh=mesh,
        in_specs=placed,
        out_specs=(P(("rows", "cols"), None), P(("cols", "rows"), None), P()),
        check_vma=False,
    )
```
